32 devices in a mesh: replica: 2 (over x), side: 4 (over y, core), tp: 4 (over z).
Axes of the slice: x: 2, y: 2, z: 4, core: 2. Of those that a mesh axis runs over, the one named last changes fastest.
Arguments:
- queries: bfloat16 [4096, 4096], P(('replica', 'side'), 'tp'), parts along dimension 0, may hold values from -60 to 60
- new_keys: bfloat16 [4096, 512], P(('replica', 'side')), parts along dimension 0, may hold values from -6 to 6
- new_values: bfloat16 [4096, 512], P(('replica', 'side')), parts along dimension 0, may hold values from -6 to 6
- cache_keys: bfloat16 [8, 512, 512], P(('replica', 'side'), 'tp'), parts along dimension 0, may hold values from -6 to 6
- cache_values: bfloat16 [8, 512, 512], P(('replica', 'side'), 'tp'), parts along dimension 0, may hold values from -6 to 6
- out_weight: bfloat16 [4096, 2048], P('tp'), may hold values from -0.09375 to 0.09375
- residual: bfloat16 [4096, 2048], P(('replica', 'side', 'tp')), parts along dimension 0, may hold values from -40 to 40
- norm_gain: bfloat16 [2048], replicated, may hold values from 0.099609375 to 1.8984375
- gate_weight: bfloat16 [16, 2048, 768], P(('side', 'tp')), may hold values from -0.125 to 0.125
- up_weight: bfloat16 [16, 2048, 768], P(('side', 'tp')), may hold values from -0.125 to 0.125
- down_weight: bfloat16 [16, 768, 2048], P(('side', 'tp')), may hold values from -0.21875 to 0.21875
- expert_ids: int32 [4096, 8], P(('replica', 'side', 'tp')), parts along dimension 0, may hold values from 0 to 15, all different within a row; in each aligned block of 128 rows (0 to 127, 128 to 255, ...) at most 128 rows name the same one
- numerators: int32 [4096, 8], P(('replica', 'side', 'tp')), parts along dimension 0, may hold values from 1 to 32767
Outputs:
- output: float32 [4096, 2048], P(('replica', 'side', 'tp')), parts along dimension 0
The draws below stay inside these ranges and needn't reach their ends.
There are 2 independent parts, one for each index of `replica`. The reference program is written for one: setup_inputs(seed, part) draws one part's arguments, and reference() takes and returns one part's arrays. A program takes and returns all parts, laid end to end along the dimension named above; an argument that names none is the same for every part. Nothing has to cross between parts.
Inputs may be any that keep to these rules, and one draw needn't show every extreme that they name: `expert_ids`: each row names 8 different experts. Among the rows of one device (aligned blocks of 128 rows) no expert is named by more than 128 rows, and in every draw some expert is named by exactly 128 rows of some device.
All inputs are finite; a program needn't handle non-finite values.
Results may differ from the reference program's by a relative error of at most 0.0035.
Values may be sent and summed in bfloat16 or wider, within the bound.
No kernel may reach another device: no remote copies, remote signals or barrier semaphores. Data moves between devices by JAX's collectives and lax.ppermute only.
A program may use at most 128 MiB of HBM per device.

```python
import math
import jax
import jax.numpy as jnp
import numpy as np
from jax import lax

D = 2048
FF = 768
H = 32
KV = 4
HD = 128
TOP = 8
CACHE_LEN = 512
TOK_GRP = 512
EXPERTS = 16
GROUPS = 4
TOKENS = 2048
ROWS_DEV = 128
CAP = 128


def shared_keys(key):
    base_key = jax.random.fold_in(key, 17)
    key_rows = jnp.clip(jax.random.normal(base_key, (GROUPS, CACHE_LEN, KV * HD), jnp.float32), -5.0, 5.0)
    return key_rows


def draw_cache_keys(key, part):
    return shared_keys(key).astype(jnp.bfloat16)


def draw_queries(key, part):
    base_key = jax.random.fold_in(key, 29)
    return jnp.clip(1.5 * jax.random.normal(base_key, (TOKENS, H * HD), jnp.float32), -9.0, 9.0).astype(jnp.bfloat16)


def draw_residual(key, part):
    base_key = jax.random.fold_in(key, 41)
    drawn = jnp.clip(jax.random.normal(base_key, (TOKENS, D), jnp.float32), -4.0, 4.0)
    return drawn.astype(jnp.bfloat16)


def set_ends(array, stream_key, low, high):
    place = [jax.random.randint(jax.random.fold_in(stream_key, axis), (), 0, length) for axis, length in enumerate(array.shape)]
    main_axis = array.shape.index(max(array.shape))
    next_to = place[:main_axis] + [(place[main_axis] + 1) % array.shape[main_axis]] + place[main_axis + 1:]
    return array.at[tuple(place)].set(low).at[tuple(next_to)].set(high)


def steps_of(rng, extent, shards, least, top_value):
    def one(axis_at, shards_of):
        heights = jax.random.uniform(jax.random.fold_in(jax.random.fold_in(rng, 6), axis_at), (shards_of,), jnp.float32, least / len(shards), top_value / len(shards))
        return jnp.repeat(jnp.exp(heights), extent[axis_at] // shards_of).reshape((-1,) + (1,) * (len(extent) - axis_at - 1))

    gain = one(*shards[0])
    for cut in shards[1:]:
        gain = gain * one(*cut)
    return gain


def deal_out(key, own, number, rows, count, top, reach, lean):
    ranking = jax.random.permutation(key, count)
    crowded, common = load_shares(count, rows * top, reach, lean, True), load_shares(count, rows * top, reach, lean, False)
    places = jnp.arange(count)

    def named(tallies, rotation):
        used = int((tallies > 0).sum())
        fixed = max(1, used // 4)
        moved = fixed + (places - fixed + rotation * (used - fixed)) % max(1, count - fixed)
        return jnp.zeros((count,), jnp.int32).at[ranking[jnp.where(places < fixed, places, moved)]].set(jnp.asarray(tallies, jnp.int32))

    tallies = jnp.where(number % 4 == 0, named(crowded, number // 4), named(common, number - number // 4 - 1))
    mixed = jax.random.permutation(jax.random.fold_in(own, 3), count)
    giver, receiver = mixed[0:count // 2 * 2:2], mixed[1:count // 2 * 2:2]
    margin = jnp.minimum(tallies[giver] - 1, reach - tallies[receiver]) // 2
    margin = jnp.where((giver == ranking[0]) | (receiver == ranking[0]) | (tallies[receiver] == 0), 0, jnp.maximum(margin, 0))
    moved = jax.random.randint(jax.random.fold_in(own, 4), (count // 2,), 0, 1 << 20) % (margin + 1)
    tallies = tallies.at[giver].add(-moved).at[receiver].add(moved)
    labels = jnp.searchsorted(jnp.cumsum(tallies), jnp.arange(rows * top), side="right").astype(jnp.int32)
    table = labels.reshape(top, rows).T
    table = table[jax.random.permutation(jax.random.fold_in(own, 1), rows)]
    rotation = jax.random.randint(jax.random.fold_in(own, 2), (rows, 1), 0, top)
    return jnp.take_along_axis(table, (jnp.arange(top)[None, :] + rotation) % top, axis=1)


def load_shares(amount, total, limit, lean, full):
    loads = [(1 << 20) // math.isqrt(rank ** lean) + 1 for rank in range(1, amount + 1)]
    largest = limit if full else min(limit, max(-(-total // amount), total * loads[0] // sum(loads)))
    least = 1 if total - largest >= amount - 1 else 0
    given, rest = [largest] + [least] * (amount - 1), total - largest - least * (amount - 1)
    while rest > 0:
        candidates = [i for i in range(1, amount) if given[i] < largest] or [i for i in range(1, amount) if given[i] < limit]
        mass, remaining = sum([loads[i] for i in candidates]), rest
        for i in candidates:
            addition = min(limit - given[i], max(1, remaining * loads[i] // mass), rest)
            given[i] = given[i] + addition
            rest = rest - addition
    return np.array(given)


def noise(stream_key, dims, spread, most, pieces=(), kind=jnp.bfloat16):
    array = spread * jax.random.normal(stream_key, dims, jnp.float32)
    if pieces:
        array = array * steps_of(stream_key, dims, pieces, -0.22, 0.18)
    return jnp.clip(array, -most, most).astype(kind)


def setup_inputs(seed: int = 0, part: int = 0) -> dict:
    key_of = jax.random.split(jax.random.key(seed), 14)
    part_splits = jax.random.split(jax.random.fold_in(key_of[13], part), 14)
    queries = draw_queries(jax.random.fold_in(jax.random.fold_in(key_of[13], part), 71), part)
    new_keys = noise(part_splits[1], (TOKENS, KV * HD), 1.0, 6.0, ((0, 4),))
    new_values = noise(part_splits[2], (TOKENS, KV * HD), 1.0, 6.0, ((0, 4),))
    cache_keys = draw_cache_keys(jax.random.fold_in(jax.random.fold_in(key_of[13], part), 71), part)
    cache_values = noise(part_splits[4], (GROUPS, CACHE_LEN, KV * HD), 1.0, 6.0, ((0, 4), (1, 4)))
    out_weight = noise(key_of[5], (H * HD, D), (H * HD) ** -0.5, 0.09375, ((0, 4),))
    residual = draw_residual(jax.random.fold_in(jax.random.fold_in(key_of[13], part), 71), part)
    norm_gain = jnp.clip(1.0 + 0.18 * jax.random.normal(key_of[7], (D,), jnp.float32), 0.099609375, 1.8984375).astype(jnp.bfloat16)
    gate_weight = noise(key_of[8], (EXPERTS, D, FF), D ** -0.5, 0.125, ((0, 16),))
    up_weight = noise(key_of[9], (EXPERTS, D, FF), D ** -0.5, 0.125, ((0, 16),))
    down_weight = noise(key_of[10], (EXPERTS, FF, D), FF ** -0.5, 0.21875, ((0, 16),))
    expert_ids_keys = jax.random.split(jax.random.fold_in(part_splits[11], 1), TOKENS // ROWS_DEV)
    expert_ids_turns = jax.random.permutation(jax.random.fold_in(part_splits[11], 3), TOKENS // ROWS_DEV)
    expert_ids = jax.vmap(lambda own, number: deal_out(jax.random.fold_in(part_splits[11], 2), own, number, ROWS_DEV, EXPERTS, TOP, CAP, 2))(expert_ids_keys, expert_ids_turns).reshape((TOKENS, TOP))
    numerators = set_ends(jax.random.randint(part_splits[12], (TOKENS, TOP), 1, 32768), jax.random.fold_in(part_splits[12], 1), 1, 32767).astype(jnp.int32)
    return dict(queries=queries, new_keys=new_keys, new_values=new_values, cache_keys=cache_keys, cache_values=cache_values, out_weight=out_weight, residual=residual, norm_gain=norm_gain, gate_weight=gate_weight, up_weight=up_weight, down_weight=down_weight, expert_ids=expert_ids, numerators=numerators)


def attend_group(operands):
    group_queries, group_keys, group_values, stored_keys, stored_values = operands
    kv_repeat = H // KV
    key_rows = jnp.concatenate([stored_keys, group_keys], axis=0).reshape(CACHE_LEN + TOK_GRP, KV, HD)
    value_rows = jnp.concatenate([stored_values, group_values], axis=0).reshape(CACHE_LEN + TOK_GRP, KV, HD)
    key_rows = jnp.repeat(key_rows, kv_repeat, axis=1).astype(jnp.float32)
    value_rows = jnp.repeat(value_rows, kv_repeat, axis=1).astype(jnp.float32)
    query_heads = group_queries.reshape(TOK_GRP, H, HD).astype(jnp.float32)
    scores = jnp.einsum('rhd,nhd->hrn', query_heads, key_rows, precision=lax.Precision.HIGHEST) / math.sqrt(HD)
    position = jnp.arange(TOK_GRP)[:, None]
    column = jnp.arange(CACHE_LEN + TOK_GRP)[None, :]
    visible = column <= position + CACHE_LEN
    scores = jnp.where(visible[None], scores, -1e+30)
    highest = lax.optimization_barrier(jnp.max(scores, axis=-1, keepdims=True))
    exponent = jnp.exp(scores - highest)
    totals = lax.optimization_barrier(jnp.sum(exponent, axis=-1))
    probs = lax.optimization_barrier(exponent.astype(jnp.bfloat16)).astype(jnp.float32)
    context = jnp.einsum('hrn,nhd->hrd', probs, value_rows, precision=lax.Precision.HIGHEST) / totals[..., None]
    return context.transpose(1, 0, 2).reshape(TOK_GRP, H * HD).astype(jnp.bfloat16)

def reference(queries, new_keys, new_values, cache_keys, cache_values, out_weight, residual, norm_gain, gate_weight, up_weight, down_weight, expert_ids, numerators):
    grouped = lax.map(attend_group, (queries.reshape(GROUPS, TOK_GRP, H * HD), new_keys.reshape(GROUPS, TOK_GRP, KV * HD), new_values.reshape(GROUPS, TOK_GRP, KV * HD), cache_keys, cache_values))
    context_all = grouped.reshape(TOKENS, H * HD)
    stream = residual.astype(jnp.float32) + jnp.dot(context_all, out_weight, preferred_element_type=jnp.float32)
    normed = (stream * lax.rsqrt(lax.optimization_barrier(jnp.mean(stream * stream, axis=-1, keepdims=True)) + 1e-06) * norm_gain.astype(jnp.float32)).astype(jnp.bfloat16)
    tile_rows = 128
    copies = TOKENS * TOP
    flat_ids = expert_ids.reshape(copies).astype(jnp.int32)
    owners = (jnp.arange(copies) // TOP).astype(jnp.int32)
    sort_order = jnp.argsort(flat_ids, stable=True).astype(jnp.int32)
    sorted_ids = flat_ids[sort_order]
    counts = jnp.zeros((EXPERTS,), jnp.int32).at[flat_ids].add(1)
    starts = (jnp.cumsum(counts) - counts).astype(jnp.int32)
    slot_rank = (jnp.arange(copies).astype(jnp.int32) - starts[sorted_ids]).astype(jnp.int32)
    padded = ((counts + tile_rows - 1) // tile_rows * tile_rows).astype(jnp.int32)
    tile_start = (jnp.cumsum(padded) - padded).astype(jnp.int32)
    placed_at = (tile_start[sorted_ids] + slot_rank).astype(jnp.int32)
    tile_count = (copies + tile_rows - 1) // tile_rows + EXPERTS
    source = jnp.zeros((tile_count * tile_rows,), jnp.int32).at[placed_at].set(owners[sort_order])
    tile_first = (jnp.arange(tile_count) * tile_rows).astype(jnp.int32)
    tile_expert = (lax.optimization_barrier(jnp.sum((tile_start[None, :] <= tile_first[:, None]).astype(jnp.int32), axis=1)) - 1).astype(jnp.int32)

    def run_tile(tile_args):
        sources, expert = tile_args
        selected = normed[sources]
        gate_sum = jnp.dot(selected, gate_weight[expert], preferred_element_type=jnp.float32)
        up_sum = jnp.dot(selected, up_weight[expert], preferred_element_type=jnp.float32)
        hidden = (jax.nn.silu(gate_sum) * up_sum).astype(jnp.bfloat16)
        return jnp.dot(hidden, down_weight[expert], preferred_element_type=jnp.float32).astype(jnp.bfloat16)
    tile_outputs = lax.map(run_tile, (source.reshape(tile_count, tile_rows), tile_expert))
    results = tile_outputs.reshape(tile_count * tile_rows, D)[placed_at]
    per_copy = jnp.zeros((copies, D), jnp.bfloat16).at[sort_order].set(results)
    weights = numerators.astype(jnp.float32)
    weights = weights / lax.optimization_barrier(jnp.sum(weights, axis=1, keepdims=True))
    mixture = lax.optimization_barrier(jnp.sum(weights[:, :, None] * per_copy.reshape(TOKENS, TOP, D).astype(jnp.float32), axis=1))
    return stream + mixture
```

```python
import functools
import math

import jax
import jax.numpy as jnp
from jax import lax
from jax.experimental import pallas as pl
from jax.experimental.pallas import tpu as pltpu
from jax.sharding import PartitionSpec as P

D = 2048
H = 32
KV = 4
HD = 128
LANES = 128
LOG2E = 1.4426950408889634
F32 = jnp.float32
BF16 = jnp.bfloat16


def contract(a, b, dims):
    return lax.dot_general(a, b, (dims, ((), ())), preferred_element_type=F32)


def vmem(count):
    return [pl.BlockSpec(memory_space=pltpu.VMEM)] * count


def pack_kernel(count, width, z_ref, *refs):
    keys, values, outs = refs[:count], refs[count : 2 * count], refs[2 * count :]
    for k_ref, v_ref, out in zip(keys, values, outs):
        out[:, :width] = k_ref[0]
        out[:, width:] = v_ref[0]


def pack_cache(z, cache_keys, cache_values, tp, width, block_of):
    positions = cache_keys.shape[1]

    def spec(d):
        return pl.BlockSpec((1, positions, width), lambda i, z_ref: (0, 0, block_of((z_ref[0] + d) % tp)))

    out_shape = jax.ShapeDtypeStruct((positions, 2 * width), BF16)
    return pl.pallas_call(
        functools.partial(pack_kernel, tp, width),
        grid_spec=pltpu.PrefetchScalarGridSpec(
            num_scalar_prefetch=1,
            grid=(1,),
            in_specs=[spec(d) for d in range(tp)] * 2,
            out_specs=[pl.BlockSpec((positions, 2 * width), lambda i, z_ref: (0, 0))] * tp,
        ),
        out_shape=[out_shape] * tp,
        name="pack_cache",
    )(z, *([cache_keys] * tp), *([cache_values] * tp))


def new_kernel(heads, per_kv, tile, scale2, z_ref, q_ref, k_ref, v_ref, acc_ref, top_ref, total_ref):
    rows = q_ref.shape[0]
    for start in range(0, rows, tile):
        seen = start + tile
        lane = lax.broadcasted_iota(jnp.int32, (tile, LANES), 1)
        tops = jnp.zeros((tile, LANES), F32)
        totals = jnp.zeros((tile, LANES), F32)
        row = lax.broadcasted_iota(jnp.int32, (tile, seen), 0) + start
        col = lax.broadcasted_iota(jnp.int32, (tile, seen), 1)
        visible = col <= row
        for h in range(heads):
            kv = slice(h // per_kv * HD, (h // per_kv + 1) * HD)
            mine = slice(h * HD, (h + 1) * HD)
            scores = contract(q_ref[start:seen, mine], k_ref[:seen, kv], ((1,), (1,))) * scale2
            scores = jnp.where(visible, scores, -1e30)
            top = jnp.max(scores, axis=-1, keepdims=True)
            exponent = jnp.exp2(scores - top)
            total = jnp.sum(exponent, axis=-1, keepdims=True)
            acc_ref[start:seen, mine] = contract(exponent.astype(BF16), v_ref[:seen, kv], ((1,), (0,)))
            tops = jnp.where(lane == h, top, tops)
            totals = jnp.where(lane == h, total, totals)
        top_ref[start:seen, :] = tops
        total_ref[start:seen, :] = totals


def attend_new(z, queries, new_keys, new_values, heads, per_kv, width, block_of, tile, scale2):
    rows = queries.shape[0]
    kv_spec = pl.BlockSpec((rows, width), lambda i, z_ref: (0, block_of(z_ref[0])))

    def whole(columns):
        return pl.BlockSpec((rows, columns), lambda i, z_ref: (0, 0))

    return pl.pallas_call(
        functools.partial(new_kernel, heads, per_kv, tile, scale2),
        grid_spec=pltpu.PrefetchScalarGridSpec(
            num_scalar_prefetch=1,
            grid=(1,),
            in_specs=[whole(heads * HD), kv_spec, kv_spec],
            out_specs=[whole(heads * HD), whole(LANES), whole(LANES)],
        ),
        out_shape=[
            jax.ShapeDtypeStruct((rows, heads * HD), F32),
            jax.ShapeDtypeStruct((rows, LANES), F32),
            jax.ShapeDtypeStruct((rows, LANES), F32),
        ],
        cost_estimate=pl.CostEstimate(flops=2 * rows * rows * HD * heads, transcendentals=rows * rows * heads, bytes_accessed=6 << 20),
        name="attend_new",
    )(z, queries, new_keys, new_values)


def cached_kernel(heads, per_kv, width, scale2, pieces, z_ref, q_ref, acc_ref, top_ref, total_ref, w_ref, *refs):
    kv_refs, out_ref, kv_all, context = refs[:pieces], refs[pieces], refs[pieces + 1], refs[pieces + 2]
    positions = kv_refs[0].shape[0]

    @pl.when(pl.program_id(0) == 0)
    def _():
        for i, ref in enumerate(kv_refs):
            kv_all[i * positions : (i + 1) * positions, :] = ref[...]

    for h in range(heads):
        kv = h // per_kv * HD
        mine = slice(h * HD, (h + 1) * HD)
        scores = contract(q_ref[:, mine], kv_all[:, kv : kv + HD], ((1,), (1,))) * scale2
        top_new = top_ref[:, h : h + 1]
        top = jnp.maximum(jnp.max(scores, axis=-1, keepdims=True), top_new)
        exponent = jnp.exp2(scores - top)
        factor = jnp.exp2(top_new - top)
        total = jnp.sum(exponent, axis=-1, keepdims=True) + total_ref[:, h : h + 1] * factor
        summed = contract(exponent.astype(BF16), kv_all[:, width + kv : width + kv + HD], ((1,), (0,)))
        summed = summed + acc_ref[:, mine] * factor
        context[:, mine] = (summed / total).astype(BF16)
    out_ref[0] = contract(context[...], w_ref[...], ((1,), (0,))).astype(BF16)


def attend_cached(z, queries, state, out_weight, pieces, heads, per_kv, width, scale2, tp, first, count):
    acc, top, total = state
    tile = queries.shape[0] // tp
    positions = pieces[0].shape[0]

    def rows_of(columns):
        return pl.BlockSpec((tile, columns), lambda i, z_ref: ((z_ref[0] + 2 * tp - first - i) % tp, 0))

    def fixed(shape):
        return pl.BlockSpec(shape, lambda i, z_ref: (0, 0))

    return pl.pallas_call(
        functools.partial(cached_kernel, heads, per_kv, width, scale2, len(pieces)),
        grid_spec=pltpu.PrefetchScalarGridSpec(
            num_scalar_prefetch=1,
            grid=(count,),
            in_specs=[rows_of(heads * HD), rows_of(heads * HD), rows_of(LANES), rows_of(LANES), fixed(out_weight.shape)]
            + [fixed(piece.shape) for piece in pieces],
            out_specs=pl.BlockSpec((1, tile, D), lambda i, z_ref: (i, 0, 0)),
            scratch_shapes=[
                pltpu.VMEM((len(pieces) * positions, 2 * width), BF16),
                pltpu.VMEM((tile, heads * HD), BF16),
            ],
        ),
        out_shape=jax.ShapeDtypeStruct((count, tile, D), BF16),
        cost_estimate=pl.CostEstimate(
            flops=2 * count * tile * heads * HD * D, transcendentals=count * tile * 512 * heads, bytes_accessed=6 << 20
        ),
        name="attend_cached",
    )(z, queries, acc, top, total, out_weight, *pieces)


def norm_kernel(experts, res_ref, own_ref, got_ref, gain_ref, ids_ref, num_ref, block_ref, stream_ref):
    stream = res_ref[...].astype(F32) + (own_ref[...].astype(F32) + got_ref[...].astype(F32))
    stream_ref[...] = stream
    mean = jnp.mean(stream * stream, axis=-1, keepdims=True)
    block_ref[:, :D] = (stream * lax.rsqrt(mean + 1e-06) * gain_ref[...].astype(F32)).astype(BF16)
    rows, extra = stream.shape[0], block_ref.shape[1] - D
    weights = num_ref[...].astype(F32)
    weights = weights / jnp.sum(weights, axis=1, keepdims=True)
    lane = lax.broadcasted_iota(jnp.int32, (rows, extra), 1)
    expert = lax.rem(lane, experts)
    table = jnp.zeros((rows, extra), F32)
    for k in range(ids_ref.shape[1]):
        table = table + jnp.where(expert == ids_ref[:, k : k + 1], weights[:, k : k + 1], 0.0)
    high = table.astype(BF16).astype(F32)
    middle = (table - high).astype(BF16).astype(F32)
    low = table - high - middle
    third = lax.div(lane, experts)
    table = jnp.where(third == 0, high, jnp.where(third == 1, middle, jnp.where(third == 2, low, 0.0)))
    block_ref[:, D:] = table.astype(BF16)


def norm_block(residual, own, got, norm_gain, expert_ids, numerators, experts):
    rows = residual.shape[0]
    extra = -(-3 * experts // LANES) * LANES
    return pl.pallas_call(
        functools.partial(norm_kernel, experts),
        in_specs=vmem(6),
        out_specs=vmem(2),
        out_shape=[jax.ShapeDtypeStruct((rows, D + extra), BF16), jax.ShapeDtypeStruct((rows, D), F32)],
        name="norm_block",
    )(residual, own, got, norm_gain.reshape(1, D), expert_ids, numerators)


def expert_kernel(count, experts, tile, e_ref, *refs):
    blocks = refs[:count]
    gate_ref, up_ref, down_ref, keep_ref, send_ref, rows_all, weight_all = refs[count:]
    rows = blocks[0].shape[0]
    extra = blocks[0].shape[1] - D
    mine = lax.rem(lax.broadcasted_iota(jnp.int32, (rows, extra), 1), experts) == e_ref[0]
    for i, ref in enumerate(blocks):
        rows_all[i * rows : (i + 1) * rows, :] = ref[:, :D]
        weight = jnp.sum(jnp.where(mine, ref[:, D:].astype(F32), 0.0), axis=-1, keepdims=True)
        weight_all[i * rows : (i + 1) * rows, :] = jnp.broadcast_to(weight, (rows, LANES))
    half = count // 2 * rows

    def results(start):
        here = rows_all[pl.ds(start, tile), :]
        gate = contract(here, gate_ref[0], ((1,), (0,)))
        up = contract(here, up_ref[0], ((1,), (0,)))
        hidden = (gate / (1.0 + jnp.exp(-gate)) * up).astype(BF16)
        out = contract(hidden, down_ref[0], ((1,), (0,))).astype(BF16).astype(F32)
        return (out * weight_all[pl.ds(start, tile), :1]).astype(BF16)

    def step(i, carry):
        start = pl.multiple_of(i * tile, tile)
        keep_ref[pl.ds(start, tile), :] = results(start)
        send_ref[pl.ds(start, tile), :] = results(start + half)
        return carry

    lax.fori_loop(0, half // tile, step, 0)


def run_expert(e, blocks, gate_weight, up_weight, down_weight, experts):
    count, rows = len(blocks), blocks[0].shape[0]
    half = count // 2 * rows
    hidden = gate_weight.shape[2]
    out_shape = jax.ShapeDtypeStruct((half, D), BF16)
    return pl.pallas_call(
        functools.partial(expert_kernel, count, experts, min(256, half)),
        in_specs=[pl.BlockSpec(memory_space=pltpu.SMEM)] + vmem(count + 3),
        out_specs=vmem(2),
        out_shape=[out_shape, out_shape],
        scratch_shapes=[pltpu.VMEM((count * rows, D), BF16), pltpu.VMEM((count * rows, LANES), F32)],
        cost_estimate=pl.CostEstimate(
            flops=6 * count * rows * D * hidden, transcendentals=count * rows * hidden, bytes_accessed=16 << 20
        ),
        name="run_expert",
    )(e, *blocks, gate_weight, up_weight, down_weight)


def ring(size, stride=1, inner=1):
    total = size * inner
    return [(i, (i // inner + stride) % size * inner + i % inner) for i in range(total)]


def add(a, b):
    return (a.astype(F32) + b.astype(F32)).astype(BF16)


def dense_experts(block, stream, gate_weight, up_weight, down_weight, tp, side):
    experts = side * tp
    cores = 2 if side % 2 == 0 else 1
    ny = side // cores
    rows = block.shape[0]
    e = (lax.axis_index("side") * tp + lax.axis_index("tp")).astype(jnp.int32).reshape(1)

    def along_z(x):
        return lax.ppermute(x, "tp", ring(tp))

    def along_y(x):
        return lax.ppermute(x, "side", ring(ny, 1, cores))

    def across(x):
        return lax.ppermute(x, "side", [(i, i ^ 1) for i in range(side)])

    planes = []
    for dz in range(tp):
        if dz:
            block = along_z(block)
        mine = [block]
        for _ in range(1, ny):
            mine.append(along_y(mine[-1]))
        planes.append(mine)
    sums = []
    for mine in planes:
        others = [across(x) for x in mine] if cores == 2 else []
        if cores == 2:
            keep, send = run_expert(e, mine + others, gate_weight, up_weight, down_weight, experts)
            got = across(send)
        parts = [add(keep[i * rows : (i + 1) * rows], got[i * rows : (i + 1) * rows]) for i in range(ny)]
        total = None
        for dy in list(range(1, ny)) + [0]:
            total = parts[dy] if total is None else add(parts[dy], along_y(total))
        sums.append(total)
    moving = None
    for dz in range(1, tp):
        moving = sums[dz] if moving is None else add(sums[dz], along_z(moving))
    return stream + (sums[0].astype(F32) + along_z(moving).astype(F32))


def routed_experts(normed, stream, gate_weight, up_weight, down_weight, expert_ids, numerators, capacity, experts_all):
    own_rows, top_count = expert_ids.shape
    copies = own_rows * top_count
    flat_ids = expert_ids.reshape(copies)
    one_hot = (flat_ids[:, None] == jnp.arange(experts_all)[None, :]).astype(jnp.int32)
    earlier = jnp.cumsum(one_hot, axis=0) - one_hot
    slot_rank = jnp.sum(earlier * one_hot, axis=1)
    slot_index = flat_ids * capacity + slot_rank
    owners = jnp.arange(copies) // top_count
    outgoing = jnp.zeros((experts_all * capacity, D), BF16).at[slot_index].set(normed[owners])
    outgoing = outgoing.reshape(experts_all, capacity, D)
    buffer = lax.all_to_all(outgoing, ("side", "tp"), split_axis=0, concat_axis=0, tiled=True)
    flat_rows = buffer.reshape(-1, D)
    gate_sum = jnp.dot(flat_rows, gate_weight[0], preferred_element_type=F32)
    upward = jnp.dot(flat_rows, up_weight[0], preferred_element_type=F32)
    hidden = (jax.nn.silu(gate_sum) * upward).astype(BF16)
    returned = lax.all_to_all(
        jnp.dot(hidden, down_weight[0], preferred_element_type=F32).astype(BF16).reshape(buffer.shape),
        ("side", "tp"),
        split_axis=0,
        concat_axis=0,
        tiled=True,
    )
    gathered = returned.reshape(experts_all * capacity, D)[slot_index]
    weights = numerators.astype(F32)
    weights = weights / jnp.sum(weights, axis=1, keepdims=True)
    mixture = jnp.sum(weights[:, :, None] * gathered.reshape(own_rows, top_count, D).astype(F32), axis=1)
    return stream + mixture


def local(
    queries,
    new_keys,
    new_values,
    cache_keys,
    cache_values,
    out_weight,
    residual,
    norm_gain,
    gate_weight,
    up_weight,
    down_weight,
    expert_ids,
    numerators,
):
    tp = lax.axis_size("tp")
    side = lax.axis_size("side")
    z = lax.axis_index("tp").astype(jnp.int32).reshape(1)
    heads = queries.shape[1] // HD
    group = H // KV
    kv_count = max(1, heads // group)
    per_kv = heads // kv_count
    width = kv_count * HD
    own_rows = residual.shape[0]
    scale2 = LOG2E / math.sqrt(HD)

    def block_of(device):
        return device * heads // group // kv_count

    packed = pack_cache(z, cache_keys, cache_values, tp, width, block_of)
    pieces = [packed[0]] + [lax.ppermute(packed[d], "tp", ring(tp, d)) for d in range(1, tp)]
    state = attend_new(z, queries, new_keys, new_values, heads, per_kv, width, block_of, own_rows, scale2)
    attend = functools.partial(attend_cached, z, queries, state, out_weight, pieces, heads, per_kv, width, scale2, tp)
    moving = attend(1, 1)[0]
    partial = attend(2, tp - 1)
    for dz in range(2, tp):
        moving = add(partial[dz - 2], lax.ppermute(moving, "tp", ring(tp)))
    got = lax.ppermute(moving, "tp", ring(tp))
    experts = side * tp
    capacity = max(2, 2 * own_rows * expert_ids.shape[1] // experts)
    block, stream = norm_block(residual, partial[tp - 2], got, norm_gain, expert_ids, numerators, experts)
    weights = (gate_weight, up_weight, down_weight)
    if capacity >= own_rows and side % 2 == 0:
        return dense_experts(block, stream, *weights, tp, side)
    return routed_experts(block[:, :D], stream, *weights, expert_ids, numerators, capacity, experts)


def solution(mesh):
    in_specs = (
        P(("replica", "side"), "tp"),
        P(("replica", "side"), None),
        P(("replica", "side"), None),
        P(("replica", "side"), "tp", None),
        P(("replica", "side"), "tp", None),
        P("tp", None),
        P(("replica", "side", "tp"), None),
        P(),
        P(("side", "tp"), None, None),
        P(("side", "tp"), None, None),
        P(("side", "tp"), None, None),
        P(("replica", "side", "tp"), None),
        P(("replica", "side", "tp"), None),
    )
    out_specs = P(("replica", "side", "tp"), None)
    return jax.shard_map(local, mesh=mesh, in_specs=in_specs, out_specs=out_specs, check_vma=False)
```

```python
import functools
import math

import jax
import jax.numpy as jnp
from jax import lax
from jax.experimental import pallas as pl
from jax.experimental.pallas import tpu as pltpu
from jax.sharding import PartitionSpec as P

D = 2048
H = 32
KV = 4
HD = 128
LANES = 128
LOG2E = 1.4426950408889634
VMEM_LIMIT = 12 << 20
F32 = jnp.float32
BF16 = jnp.bfloat16


def contract(a, b, dims):
    return lax.dot_general(a, b, (dims, ((), ())), preferred_element_type=F32)


def vmem(count):
    return [pl.BlockSpec(memory_space=pltpu.VMEM)] * count


def pinned(arrays):
    return [pltpu.with_memory_space_constraint(x, pltpu.VMEM) for x in arrays]


def pack_kernel(count, width, block_of, place_ref, keys_ref, values_ref, *refs):
    outs, sems = refs[:count], refs[count]
    copies = []
    for d, out in enumerate(outs):
        start = pl.multiple_of(block_of(lax.rem(place_ref[0] + d, count)) * width, LANES)
        for i, ref in enumerate((keys_ref, values_ref)):
            source = ref.at[0, :, pl.ds(start, width)]
            copies.append(pltpu.make_async_copy(source, out.at[:, i * width : (i + 1) * width], sems.at[d, i]))
    for copy in copies:
        copy.start()
    for copy in copies:
        copy.wait()


def pack_cache(place, cache_keys, cache_values, tp, width, block_of):
    positions = cache_keys.shape[1]
    caches = [pltpu.with_memory_space_constraint(x, pltpu.HBM) for x in (cache_keys, cache_values)]
    return pl.pallas_call(
        functools.partial(pack_kernel, tp, width, block_of),
        in_specs=[pl.BlockSpec(memory_space=pltpu.SMEM)] + [pl.BlockSpec(memory_space=pl.ANY)] * 2,
        out_specs=vmem(tp),
        out_shape=[pltpu.VMEM((positions, 2 * width), BF16)] * tp,
        scratch_shapes=[pltpu.SemaphoreType.DMA((tp, 2))],
        compiler_params=pltpu.CompilerParams(vmem_limit_bytes=2 << 20),
        name="pack_cache",
    )(place, *caches)


def attend_kernel(heads, per_kv, width, scale2, pieces, tp, first, place_ref, q_ref, k_ref, v_ref, w_ref, *refs):
    kv_refs = refs[:pieces]
    k_all, v_all, bias, context = refs[-4:]
    out_refs = refs[pieces:-4]
    rows, tile = k_ref.shape[0], q_ref.shape[0]
    positions = kv_refs[0].shape[0]
    step = pl.program_id(0)

    @pl.when(step == 0)
    def _():
        for i, ref in enumerate(kv_refs):
            k_all[i * positions : (i + 1) * positions, :] = ref[:, :width]
            v_all[i * positions : (i + 1) * positions, :] = ref[:, width:]
        k_all[pieces * positions :, :] = k_ref[...]
        v_all[pieces * positions :, :] = v_ref[...]

    start = lax.rem(place_ref[0] + 2 * tp - first - step, tp) * tile
    row = lax.broadcasted_iota(jnp.int32, (tile, rows), 0) + start
    col = lax.broadcasted_iota(jnp.int32, (tile, rows), 1)
    bias[...] = jnp.where(col <= row, 0.0, -1e30)
    pair = 2 if per_kv % 2 == 0 else 1
    cached = pieces * positions
    for h in range(0, heads, pair):
        kv = slice(h // per_kv * HD, (h // per_kv + 1) * HD)
        query = jnp.concatenate([q_ref[:, (h + i) * HD : (h + i + 1) * HD] for i in range(pair)], axis=0)
        older = contract(query, k_all[:cached, kv], ((1,), (1,)))
        newer = contract(query, k_all[cached:, kv], ((1,), (1,)))
        newer = (newer.reshape(pair, tile, rows) + bias[...][None]).reshape(pair * tile, rows)
        top = jnp.maximum(jnp.max(older, axis=-1, keepdims=True), jnp.max(newer, axis=-1, keepdims=True))
        older = jnp.exp2((older - top) * scale2)
        newer = jnp.exp2((newer - top) * scale2)
        total = jnp.sum(older, axis=-1, keepdims=True) + jnp.sum(newer, axis=-1, keepdims=True)
        summed = contract(older.astype(BF16), v_all[:cached, kv], ((1,), (0,)))
        summed = summed + contract(newer.astype(BF16), v_all[cached:, kv], ((1,), (0,)))
        done = (summed / total).astype(BF16)
        for i in range(pair):
            context[:, (h + i) * HD : (h + i + 1) * HD] = done[i * tile : (i + 1) * tile]
    out = contract(context[...], w_ref[...], ((1,), (0,))).astype(BF16)
    size = tile // len(out_refs)
    for i, ref in enumerate(out_refs):
        ref[0] = out[i * size : (i + 1) * size]


def attend(place, queries, new_keys, new_values, out_weight, pieces, heads, per_kv, width, block_of, scale2, tp, streams, first, count):
    rows = queries.shape[0]
    tile = rows // tp
    positions = pieces[0].shape[0]
    kv_spec = pl.BlockSpec((rows, width), lambda i, place_ref: (0, block_of(place_ref[0])))
    q_spec = pl.BlockSpec((tile, heads * HD), lambda i, place_ref: ((place_ref[0] + 2 * tp - first - i) % tp, 0))

    def fixed(shape):
        return pl.BlockSpec(shape, lambda i, place_ref: (0, 0))

    keys = len(pieces) * positions + rows
    return pl.pallas_call(
        functools.partial(attend_kernel, heads, per_kv, width, scale2, len(pieces), tp, first),
        grid_spec=pltpu.PrefetchScalarGridSpec(
            num_scalar_prefetch=1,
            grid=(count,),
            in_specs=[q_spec, kv_spec, kv_spec, fixed(out_weight.shape)] + [fixed(piece.shape) for piece in pieces],
            out_specs=[pl.BlockSpec((1, tile // streams, D), lambda i, place_ref: (i, 0, 0))] * streams,
            scratch_shapes=[
                pltpu.VMEM((keys, width), BF16),
                pltpu.VMEM((keys, width), BF16),
                pltpu.VMEM((tile, rows), F32),
                pltpu.VMEM((tile, heads * HD), BF16),
            ],
        ),
        out_shape=[pltpu.VMEM((count, tile // streams, D), BF16)] * streams,
        cost_estimate=pl.CostEstimate(
            flops=2 * count * tile * heads * HD * (D + 2 * keys),
            transcendentals=count * tile * keys * heads,
            bytes_accessed=6 << 20,
        ),
        compiler_params=pltpu.CompilerParams(vmem_limit_bytes=VMEM_LIMIT),
        name="attend",
    )(place, *pinned([queries, new_keys, new_values, out_weight, *pieces]))


def norm_kernel(experts, part, res_ref, own_ref, got_ref, gain_ref, ids_ref, num_ref, block_ref, stream_ref):
    rows = got_ref.shape[0]
    here = slice(part * rows, (part + 1) * rows)
    stream = res_ref[here].astype(F32) + (own_ref[own_ref.shape[0] - 1].astype(F32) + got_ref[...].astype(F32))
    stream_ref[...] = stream
    mean = jnp.mean(stream * stream, axis=-1, keepdims=True)
    block_ref[:, :D] = (stream * lax.rsqrt(mean + 1e-06) * gain_ref[...].astype(F32)).astype(BF16)
    extra = block_ref.shape[1] - D
    weights = num_ref[...].astype(F32)
    weights = (weights / jnp.sum(weights, axis=0, keepdims=True)).T[here]
    ids = ids_ref[...].T[here]
    lane = lax.broadcasted_iota(jnp.int32, (rows, extra), 1)
    expert = lax.rem(lane, experts)
    table = jnp.zeros((rows, extra), F32)
    for k in range(ids_ref.shape[0]):
        table = table + jnp.where(expert == ids[:, k : k + 1], weights[:, k : k + 1], 0.0)
    high = table.astype(BF16).astype(F32)
    middle = (table - high).astype(BF16).astype(F32)
    low = table - high - middle
    third = lax.div(lane, experts)
    table = jnp.where(third == 0, high, jnp.where(third == 1, middle, jnp.where(third == 2, low, 0.0)))
    block_ref[:, D:] = table.astype(BF16)


def norm_block(part, residual, own, got, norm_gain, expert_ids, numerators, experts):
    rows = got.shape[0]
    extra = -(-3 * experts // LANES) * LANES
    return pl.pallas_call(
        functools.partial(norm_kernel, experts, part),
        in_specs=vmem(6),
        out_specs=vmem(2),
        out_shape=[pltpu.VMEM((rows, D + extra), BF16), pltpu.VMEM((rows, D), F32)],
        compiler_params=pltpu.CompilerParams(vmem_limit_bytes=VMEM_LIMIT),
        name="norm_block",
    )(*pinned([residual, own, got, norm_gain, expert_ids, numerators]))


def expert_kernel(count, experts, tile, place_ref, *refs):
    blocks = refs[:count]
    gate_ref, up_ref, down_ref, keep_ref, send_ref, rows_all, weight_all = refs[count:]
    rows = blocks[0].shape[0]
    extra = blocks[0].shape[1] - D
    mine = lax.rem(lax.broadcasted_iota(jnp.int32, (rows, extra), 1), experts) == place_ref[1]
    for i, ref in enumerate(blocks):
        rows_all[i * rows : (i + 1) * rows, :] = ref[:, :D]
        weight = jnp.sum(jnp.where(mine, ref[:, D:].astype(F32), 0.0), axis=-1, keepdims=True)
        weight_all[i * rows : (i + 1) * rows, :] = jnp.broadcast_to(weight, (rows, LANES))
    half = count // 2 * rows
    for start in range(0, count * rows, tile):
        here = rows_all[start : start + tile, :]
        gate = contract(here, gate_ref[0], ((1,), (0,)))
        up = contract(here, up_ref[0], ((1,), (0,)))
        hidden = (gate / (1.0 + jnp.exp(-gate)) * up).astype(BF16)
        out = contract(hidden, down_ref[0], ((1,), (0,))).astype(BF16).astype(F32)
        out = (out * weight_all[start : start + tile, :1]).astype(BF16)
        size = min(tile, half)
        for i in range(0, tile, size):
            to, at = (keep_ref, start + i) if start + i < half else (send_ref, start + i - half)
            to[at : at + size, :] = out[i : i + size]


def run_expert(place, blocks, gate_weight, up_weight, down_weight, experts):
    count, rows = len(blocks), blocks[0].shape[0]
    half = count // 2 * rows
    hidden = gate_weight.shape[2]
    out_shape = pltpu.VMEM((half, D), BF16)
    return pl.pallas_call(
        functools.partial(expert_kernel, count, experts, min(256, count * rows)),
        in_specs=[pl.BlockSpec(memory_space=pltpu.SMEM)] + vmem(count + 3),
        out_specs=vmem(2),
        out_shape=[out_shape, out_shape],
        scratch_shapes=[pltpu.VMEM((count * rows, D), BF16), pltpu.VMEM((count * rows, LANES), F32)],
        cost_estimate=pl.CostEstimate(
            flops=6 * count * rows * D * hidden, transcendentals=count * rows * hidden, bytes_accessed=16 << 20
        ),
        compiler_params=pltpu.CompilerParams(vmem_limit_bytes=VMEM_LIMIT),
        name="run_expert",
    )(place, *pinned([*blocks, gate_weight, up_weight, down_weight]))


def stage_kernel(count, *refs):
    sources, targets, sems = refs[:count], refs[-1 - count : -1], refs[-1]
    copies = [pltpu.make_async_copy(a, b, sems.at[i]) for i, (a, b) in enumerate(zip(sources, targets))]
    for copy in copies:
        copy.start()
    for copy in copies:
        copy.wait()


def stage(arrays, after):
    count = len(arrays)
    return pl.pallas_call(
        functools.partial(stage_kernel, count),
        in_specs=[pl.BlockSpec(memory_space=pl.ANY)] * (count + len(after)),
        out_specs=vmem(count),
        out_shape=[pltpu.VMEM(x.shape, x.dtype) for x in arrays],
        scratch_shapes=[pltpu.SemaphoreType.DMA((count,))],
        cost_estimate=pl.CostEstimate(flops=0, transcendentals=0, bytes_accessed=sum(2 * x.size for x in arrays)),
        compiler_params=pltpu.CompilerParams(vmem_limit_bytes=2 << 20),
        name="stage",
    )(*[pltpu.with_memory_space_constraint(x, pltpu.HBM) for x in arrays], *after)


def finish_kernel(part, base_ref, own_ref, side_ref, got_ref, *refs):
    out_ref, total, sem = refs[-3:]
    rows = total.shape[0]
    total[...] = base_ref[...] + (own_ref[:rows].astype(F32) + side_ref[...].astype(F32) + got_ref[...].astype(F32))
    copy = pltpu.make_async_copy(total, out_ref.at[pl.ds(part * rows, rows)], sem)
    copy.start()
    copy.wait()


def finish(part, streams, base, own, aside, got, out):
    rows = base.shape[0]
    return pl.pallas_call(
        functools.partial(finish_kernel, part),
        in_specs=vmem(4) + [pl.BlockSpec(memory_space=pl.ANY)] * (part > 0),
        out_specs=pl.BlockSpec(memory_space=pl.ANY),
        out_shape=jax.ShapeDtypeStruct((streams * rows, D), F32),
        scratch_shapes=[pltpu.VMEM((rows, D), F32), pltpu.SemaphoreType.DMA],
        input_output_aliases={4: 0} if part else {},
        compiler_params=pltpu.CompilerParams(vmem_limit_bytes=VMEM_LIMIT),
        name="finish",
    )(*pinned([base, own, aside, got]), *([out] if part else []))


def ring(size, stride=1, inner=1):
    total = size * inner
    return [(i, (i // inner + stride) % size * inner + i % inner) for i in range(total)]


def add(a, b):
    return (a.astype(F32) + b.astype(F32)).astype(BF16)


def dense_experts(block, stream, weights, place, tp, side):
    experts = side * tp
    cores = 2
    ny = side // cores
    rows = block.shape[0]
    hold = lax.optimization_barrier
    last = tp - 1

    def along_z(x):
        return lax.ppermute(x, "tp", ring(tp))

    def along_y(x):
        return lax.ppermute(x, "side", ring(ny, 1, cores))

    def across(x):
        return lax.ppermute(x, "side", [(i, i ^ 1) for i in range(side)])

    blocks = [[None] * ny for _ in range(tp)]
    others = [[None] * ny for _ in range(tp)]
    blocks[0][0] = block
    sent, kept, parts, joined = [None] * tp, [None] * tp, [None] * tp, [None] * tp

    def compute(dz):
        kept[dz], sent[dz] = run_expert(place, blocks[dz] + others[dz], *weights, experts)

    def halves(dz):
        got = across(sent[dz])
        parts[dz] = [add(kept[dz][i * rows : (i + 1) * rows], got[i * rows : (i + 1) * rows]) for i in range(ny)]

    def join(dz):
        total = parts[dz][1] if ny > 1 else None
        for dy in range(2, ny):
            total = add(parts[dz][dy], along_y(total))
        joined[dz] = along_y(total) if ny > 1 else None

    moving = None
    if ny == 2 and tp > 2:
        blocks[1][0], blocks[0][1], others[0][0] = hold((along_z(block), along_y(block), across(block)))
        others[0][1] = across(blocks[0][1])
        for dz in range(1, tp):
            compute(dz - 1)
            here = blocks[dz][0]
            if dz < last:
                ahead = [along_z(here), along_y(here)]
            else:
                ahead = [along_z(blocks[dz - 1][1])]
                halves(1)
                join(1)
                ahead.append(joined[1])
            others[dz][0] = across(here)
            ahead, others[dz][0], kept[dz - 1], sent[dz - 1] = hold((ahead, others[dz][0], kept[dz - 1], sent[dz - 1]))
            if dz < last:
                blocks[dz + 1][0], blocks[dz][1] = ahead
            else:
                blocks[dz][1], joined[1] = ahead
            others[dz][1] = across(blocks[dz][1])
        halves(2)
        others[last][1], parts[2] = hold((others[last][1], parts[2]))
        compute(last)
        for dz in range(2, tp + 1):
            total = add(parts[dz - 1][0], joined[dz - 1])
            moving = total if moving is None else add(total, moving)
            moving = along_z(moving)
            now = dz % tp
            if parts[now] is None:
                halves(now)
            if now == 0:
                parts[0], joined[last] = hold((parts[0], joined[last]))
            join(now)
            if dz == 2:
                moving, joined[now], kept[last], sent[last] = hold((moving, joined[now], kept[last], sent[last]))
            elif dz <= last:
                moving, joined[now] = hold((moving, joined[now]))
        return stream, parts[0][0], joined[0], moving
    for dz in range(tp):
        if dz:
            blocks[dz][0] = along_z(blocks[dz - 1][0])
        for dy in range(1, ny):
            blocks[dz][dy] = along_y(blocks[dz][dy - 1])
        others[dz] = [across(x) for x in blocks[dz]]
        compute(dz)
        halves(dz)
        join(dz)
        parts[dz] = parts[dz][0] if ny == 1 else add(parts[dz][0], joined[dz])
    for dz in range(1, tp):
        moving = parts[dz] if moving is None else add(parts[dz], along_z(moving))
    return stream, parts[0], jnp.zeros_like(parts[0]), along_z(moving)


def routed_experts(normed, stream, gate_weight, up_weight, down_weight, expert_ids, numerators, capacity, experts_all):
    own_rows, top_count = expert_ids.shape
    copies = own_rows * top_count
    flat_ids = expert_ids.reshape(copies)
    one_hot = (flat_ids[:, None] == jnp.arange(experts_all)[None, :]).astype(jnp.int32)
    earlier = jnp.cumsum(one_hot, axis=0) - one_hot
    slot_rank = jnp.sum(earlier * one_hot, axis=1)
    slot_index = flat_ids * capacity + slot_rank
    owners = jnp.arange(copies) // top_count
    outgoing = jnp.zeros((experts_all * capacity, D), BF16).at[slot_index].set(normed[owners])
    outgoing = outgoing.reshape(experts_all, capacity, D)
    buffer = lax.all_to_all(outgoing, ("side", "tp"), split_axis=0, concat_axis=0, tiled=True)
    flat_rows = buffer.reshape(-1, D)
    gate_sum = jnp.dot(flat_rows, gate_weight[0], preferred_element_type=F32)
    upward = jnp.dot(flat_rows, up_weight[0], preferred_element_type=F32)
    hidden = (jax.nn.silu(gate_sum) * upward).astype(BF16)
    returned = lax.all_to_all(
        jnp.dot(hidden, down_weight[0], preferred_element_type=F32).astype(BF16).reshape(buffer.shape),
        ("side", "tp"),
        split_axis=0,
        concat_axis=0,
        tiled=True,
    )
    gathered = returned.reshape(experts_all * capacity, D)[slot_index]
    weights = numerators.astype(F32)
    weights = weights / jnp.sum(weights, axis=1, keepdims=True)
    mixture = jnp.sum(weights[:, :, None] * gathered.reshape(own_rows, top_count, D).astype(F32), axis=1)
    return stream + mixture


def local(
    queries,
    new_keys,
    new_values,
    cache_keys,
    cache_values,
    out_weight,
    residual,
    norm_gain,
    gate_weight,
    up_weight,
    down_weight,
    expert_ids,
    numerators,
):
    tp = lax.axis_size("tp")
    side = lax.axis_size("side")
    z = lax.axis_index("tp").astype(jnp.int32)
    place = jnp.stack([z, lax.axis_index("side").astype(jnp.int32) * tp + z])
    heads = queries.shape[1] // HD
    group = H // KV
    kv_count = max(1, heads // group)
    per_kv = heads // kv_count
    width = kv_count * HD
    own_rows = residual.shape[0]
    scale2 = LOG2E / math.sqrt(HD)

    def block_of(device):
        return device * heads // group // kv_count

    experts = side * tp
    capacity = max(2, 2 * own_rows * expert_ids.shape[1] // experts)
    dense = capacity >= own_rows and side % 2 == 0
    streams = 2 if dense and own_rows % 32 == 0 else 1
    packed = pack_cache(place, cache_keys, cache_values, tp, width, block_of)
    pieces = [packed[0]] + [lax.ppermute(packed[d], "tp", ring(tp, d)) for d in range(1, tp)]
    sources = stage((queries, new_keys, new_values, out_weight), packed[:1])
    run = functools.partial(attend, place, *sources, pieces, heads, per_kv, width, block_of, scale2, tp, streams)
    moving = [part[0] for part in run(1, 1)]
    partial = run(2, tp - 1)
    weights = (gate_weight, up_weight, down_weight)
    small = (residual, norm_gain.reshape(1, D), expert_ids.T, numerators.T)
    if dense:
        *weights, residual, gain, ids, shares = stage((*weights, *small), partial[:1])
    else:
        residual, gain, ids, shares = small
    blocks, bases = [], []
    for dz in range(2, tp):
        for i in range(streams):
            moving[i] = add(partial[i][dz - 2], lax.ppermute(moving[i], "tp", ring(tp)))
    for i in range(streams):
        got = lax.ppermute(moving[i], "tp", ring(tp))
        block, base = norm_block(i, residual, partial[i], got, gain, ids, shares, experts)
        blocks.append(block)
        bases.append(base)
    if dense:
        out = None
        for i in range(streams):
            out = finish(i, streams, *dense_experts(blocks[i], bases[i], weights, place, tp, side), out)
        return out
    return routed_experts(blocks[0][:, :D], bases[0], *weights, expert_ids, numerators, capacity, experts)


def solution(mesh):
    in_specs = (
        P(("replica", "side"), "tp"),
        P(("replica", "side"), None),
        P(("replica", "side"), None),
        P(("replica", "side"), "tp", None),
        P(("replica", "side"), "tp", None),
        P("tp", None),
        P(("replica", "side", "tp"), None),
        P(),
        P(("side", "tp"), None, None),
        P(("side", "tp"), None, None),
        P(("side", "tp"), None, None),
        P(("replica", "side", "tp"), None),
        P(("replica", "side", "tp"), None),
    )
    out_specs = P(("replica", "side", "tp"), None)
    return jax.shard_map(local, mesh=mesh, in_specs=in_specs, out_specs=out_specs, check_vma=False)
```
